256 devices in a mesh: dp: 32 (over x, z), mp: 8 (over y, core).
Axes of the slice: x: 4, y: 4, z: 8, core: 2. Of those that a mesh axis runs over, the one named last changes fastest.
Arguments:
- grad_parts: bfloat16 [32, 16, 1024, 1024], P('dp', None, None, 'mp'), may hold values from -6 to 6
- owners: int32 [16], replicated, may hold values from 0 to 7, as said below
- left_stat: float32 [32, 1024, 1024], P('mp', 'dp'), may hold values from -1 to 8
- right_stat: float32 [32, 1024, 1024], P('mp', 'dp'), may hold values from -1 to 8
- left_root: bfloat16 [32, 1024, 1024], P('mp', 'dp'), may hold values from -1 to 9
- right_root: bfloat16 [32, 1024, 1024], P('mp'), may hold values from -1 to 3
- first_moment: float32 [32, 1024, 1024], P('mp', 'dp'), may hold values from -32 to 32
- second_moment: float32 [32, 1024, 1024], P('mp', 'dp'), may hold values from 0.5 to 2
- vec_grad: bfloat16 [32, 73728], P('dp', 'mp'), may hold values from -3 to 3
- vec_first: float32 [73728], P('mp'), may hold values from -4 to 4
- vec_second: float32 [73728], P('mp'), may hold values from 0.5 to 2
Outputs:
- block_update: bfloat16 [16, 1024, 1024], P(None, 'dp', 'mp')
- left_new: float32 [32, 1024, 1024], P('mp', 'dp')
- right_new: float32 [32, 1024, 1024], P('mp', 'dp')
- first_new: float32 [32, 1024, 1024], P('mp', 'dp')
- second_new: float32 [32, 1024, 1024], P('mp', 'dp')
- vec_update: bfloat16 [73728], P('mp')
- vec_first_new: float32 [73728], P('mp')
- vec_second_new: float32 [73728], P('mp')
The draws below stay inside these ranges and needn't reach their ends.
Inputs may be any that keep to these rules, and one draw needn't show every extreme that they name: `owners`: no owner holds more than 4 blocks, and in every draw some owner holds exactly 4.
All inputs are finite; a program needn't handle non-finite values.
Results may differ from the reference program's by a relative error of at most 0.018.
Values may be sent and summed in bfloat16 or wider, within the bound.
A program may use at most 128 MiB of HBM per device.

```python
import math
import jax
import jax.numpy as jnp
from jax import lax

BS = 1024
VEC = 73728
CAP = 4
NB = 16
SLOTS = 32
PARTIALS = 32
N_MP = 8


def symmetric_draw(key, diag_lo, diag_hi, off_scale, rise):
    shape = (SLOTS, BS, BS)
    key_off, key_diag = jax.random.split(key)
    base = jax.random.normal(key_off, shape, jnp.float32)
    offdiag = (base + jnp.swapaxes(base, 1, 2)) * (off_scale * 0.70710678 / math.sqrt(BS))
    rows = lax.broadcasted_iota(jnp.float32, shape, 1)
    cols = lax.broadcasted_iota(jnp.float32, shape, 2)
    spread = jax.random.uniform(key_diag, shape, jnp.float32)
    diagonal = diag_lo * jnp.exp(spread * math.log(diag_hi / diag_lo) + rows * (math.log(rise) / max(BS - 1, 1)))
    return jnp.where(rows == cols, diagonal, offdiag)


def draw_left_stat(key, part):
    return symmetric_draw(jax.random.fold_in(key, 11), 1.0, 4.0, 0.8, 1.0)


def draw_right_stat(key, part):
    return symmetric_draw(jax.random.fold_in(key, 12), 1.0, 4.0, 0.8, 1.0)


def draw_left_root(key, part):
    return symmetric_draw(jax.random.fold_in(key, 13), 0.5, 1.5, 0.8, 3.0).astype(jnp.bfloat16)


def draw_right_root(key, part):
    return symmetric_draw(jax.random.fold_in(key, 14), 0.5, 1.5, 0.8, 1.0).astype(jnp.bfloat16)


def draw_first_moment(key, part):
    shape = (SLOTS, BS, BS)
    key_base, key_cols = jax.random.split(jax.random.fold_in(key, 15), 2)
    rows = lax.broadcasted_iota(jnp.float32, shape, 1)
    row_scale = 0.3 * jnp.exp(rows * (math.log(10.0) / max(BS - 1, 1)))
    col_scale = jnp.exp(jax.random.uniform(key_cols, (SLOTS, 1, BS), jnp.float32) * math.log(3.0))
    base = jax.random.truncated_normal(key_base, -3.0, 3.0, shape, jnp.float32)
    return base * row_scale * col_scale


def draw_owners(key, part):
    key_busy, key_slots, key_order = jax.random.split(jax.random.fold_in(key, 16), 3)
    busiest = jax.random.randint(key_busy, (), 0, N_MP)
    last_first = (N_MP - 2) * CAP
    rest = jax.random.permutation(key_slots, (N_MP - 1) * CAP - 2).astype(jnp.int32) + 1
    rest = rest + (rest >= last_first).astype(jnp.int32)
    fixed = jnp.array([0, last_first], jnp.int32)
    other_slots = jnp.concatenate([fixed, rest])[:NB - CAP]
    other_owner = other_slots // CAP
    other_owner = other_owner + (other_owner >= busiest).astype(jnp.int32)
    listed = jnp.concatenate([jnp.full((CAP,), 1, jnp.int32) * busiest, other_owner.astype(jnp.int32)])
    order = jax.random.permutation(key_order, NB)
    return listed[order].astype(jnp.int32)


def raised(drawn, rng, source, target, parts, factor):
    def block_of(axis_at):
        return (jnp.arange(drawn.shape[axis_at]) // (drawn.shape[axis_at] // parts)).reshape((-1,) + (1,) * (drawn.ndim - 1 - axis_at))

    first = jax.random.permutation(rng, parts)[block_of(target)]
    other_side = (block_of(target) + parts // 2) % parts
    return jnp.where((block_of(source) == first) | (block_of(source) == other_side), factor * drawn, drawn)


def block_levels(own_key, extent, shards, low, largest):
    level = 1.0
    for axis_at, blocks in shards:
        steps = jax.random.uniform(jax.random.fold_in(jax.random.fold_in(own_key, 6), axis_at), (blocks,), jnp.float32, low / len(shards), largest / len(shards))
        level = level * jnp.repeat(jnp.exp(steps), extent[axis_at] // blocks).reshape((-1,) + (1,) * (len(extent) - 1 - axis_at))
    return level


def normal_values(own_key, extent, scale, reach, pieces=(), held_as=jnp.bfloat16):
    values = jax.random.normal(own_key, extent, jnp.float32) * scale
    if len(pieces) > 0:
        values = block_levels(own_key, extent, pieces, -0.22, 0.18) * values
    return jnp.clip(values, min=-reach, max=reach).astype(held_as)


def heavy_noise(key, shape, scale, bound, cuts, heavy, dtype=jnp.bfloat16):
    entries = scale * jax.random.normal(key, shape, jnp.float32)
    if cuts:
        entries = entries * block_levels(key, shape, cuts, -0.22, 0.18)
    return jnp.clip(raised(entries, jax.random.fold_in(key, 3), *heavy), -bound, bound).astype(dtype)


def setup_inputs(seed: int = 0) -> dict:
    streams_of = jax.random.split(jax.random.key(seed), 12)
    grad_parts = heavy_noise(streams_of[0], (PARTIALS, NB, BS, BS), 0.2, 6.0, ((0, 32), (3, 8)), (0, 2, 32, 2.75))
    owners = draw_owners(jax.random.fold_in(streams_of[11], 71), 0)
    left_stat = draw_left_stat(jax.random.fold_in(streams_of[11], 71), 0)
    right_stat = draw_right_stat(jax.random.fold_in(streams_of[11], 71), 0)
    left_root = draw_left_root(jax.random.fold_in(streams_of[11], 71), 0)
    right_root = draw_right_root(jax.random.fold_in(streams_of[11], 71), 0)
    first_moment = draw_first_moment(jax.random.fold_in(streams_of[11], 71), 0)
    second_moment = jnp.clip(jnp.exp(math.log(2.0) - 1.3862944 * jax.random.uniform(streams_of[7], (SLOTS, BS, BS), jnp.float32) ** block_levels(streams_of[7], (SLOTS, BS, BS), ((0, 8), (1, 32)), -0.2, 0.2)), 0.5, 2.0)
    vec_grad = normal_values(streams_of[8], (PARTIALS, VEC), 0.2, 3.0, ((0, 32), (1, 8)))
    vec_first = normal_values(streams_of[9], (VEC,), 0.3, 4.0, ((0, 8),), jnp.float32)
    vec_second = jnp.clip(jnp.exp(math.log(2.0) - 1.3862944 * jax.random.uniform(streams_of[10], (VEC,), jnp.float32) ** block_levels(streams_of[10], (VEC,), ((0, 8),), -0.2, 0.2)), 0.5, 2.0)
    return {"grad_parts": grad_parts, "owners": owners, "left_stat": left_stat, "right_stat": right_stat, "left_root": left_root, "right_root": right_root, "first_moment": first_moment, "second_moment": second_moment, "vec_grad": vec_grad, "vec_first": vec_first, "vec_second": vec_second}


beta_one = 0.9
beta_two = 0.95
adam_eps = 1e-08
graft_eps = 1e-06

def owner_table(owners, owner_count, slot_count):
    block_count = owners.shape[0]
    same = owners[:, None] == owners[None, :]
    earlier = lax.broadcasted_iota(jnp.int32, (block_count, block_count), 1) < lax.broadcasted_iota(jnp.int32, (block_count, block_count), 0)
    slots = lax.optimization_barrier(jnp.sum((same & earlier).astype(jnp.int32), axis=1))
    owner_ids = lax.broadcasted_iota(jnp.int32, (owner_count, slot_count, block_count), 0)
    slot_ids = lax.broadcasted_iota(jnp.int32, (owner_count, slot_count, block_count), 1)
    return ((owners[None, None, :] == owner_ids) & (slots[None, None, :] == slot_ids)).astype(jnp.float32)

def reference(grad_parts, owners, left_stat, right_stat, left_root, right_root, first_moment, second_moment, vec_grad, vec_first, vec_second):

    def add_part(which_part, running):
        return running + lax.dynamic_index_in_dim(grad_parts, which_part, 0, keepdims=False).astype(jnp.float32)
    summed = lax.fori_loop(0, PARTIALS, add_part, jnp.zeros((NB, BS, BS), jnp.float32))
    selector = owner_table(owners, N_MP, CAP)
    gathered = jnp.einsum('ocb,bij->ocij', selector, summed, precision=lax.Precision.HIGHEST).reshape(SLOTS, BS, BS)
    used = (lax.optimization_barrier(jnp.sum(selector, axis=2)) > 0.5).reshape(SLOTS, 1, 1)

    def per_slot(operands):
        grad_block, root_left, root_right = operands
        rounded = grad_block.astype(jnp.bfloat16)
        left_term = jnp.dot(rounded, rounded.T, preferred_element_type=jnp.float32)
        right_term = jnp.dot(rounded.T, rounded, preferred_element_type=jnp.float32)
        applied = jnp.dot(root_left, rounded, preferred_element_type=jnp.float32).astype(jnp.bfloat16)
        precond = jnp.dot(applied, root_right, preferred_element_type=jnp.float32)
        return (left_term, right_term, precond)
    left_term, right_term, precond = lax.map(per_slot, (gathered, left_root, right_root))
    scale = 1.0 / BS
    left_new = jnp.where(used, left_stat + left_term * scale, left_stat)
    right_new = jnp.where(used, right_stat + right_term * scale, right_stat)
    first_new = jnp.where(used, beta_one * first_moment + (1.0 - beta_one) * gathered, first_moment)
    second_new = jnp.where(used, beta_two * second_moment + (1.0 - beta_two) * gathered * gathered, second_moment)
    adam = first_new / (jnp.sqrt(second_new) + adam_eps)
    mean_adam = lax.optimization_barrier(jnp.mean(adam * adam, axis=(1, 2)))
    mean_pre = lax.optimization_barrier(jnp.mean(precond * precond, axis=(1, 2)))
    graft = jnp.sqrt(mean_adam) / jnp.sqrt(mean_pre + graft_eps)
    updates = (precond * graft[:, None, None]).astype(jnp.bfloat16)
    block_update = jnp.einsum('ocb,ocij->bij', selector, updates.astype(jnp.float32).reshape(N_MP, CAP, BS, BS), precision=lax.Precision.HIGHEST).astype(jnp.bfloat16)
    vec_sum = lax.optimization_barrier(jnp.sum(vec_grad.astype(jnp.float32), axis=0))
    vec_first_new = beta_one * vec_first + (1.0 - beta_one) * vec_sum
    vec_second_new = beta_two * vec_second + (1.0 - beta_two) * vec_sum * vec_sum
    vec_update = (vec_first_new / (jnp.sqrt(vec_second_new) + adam_eps)).astype(jnp.bfloat16)
    return (block_update, left_new, right_new, first_new, second_new, vec_update, vec_first_new, vec_second_new)
```

```python
import jax
import jax.numpy as jnp
from jax import lax
from jax.sharding import PartitionSpec as P

beta_one = 0.9
beta_two = 0.95
adam_eps = 1e-08
graft_eps = 1e-06


def owner_table(owners, owner_count, slot_count):
    block_count = owners.shape[0]
    same = owners[:, None] == owners[None, :]
    earlier = lax.broadcasted_iota(jnp.int32, (block_count, block_count), 1) < lax.broadcasted_iota(
        jnp.int32, (block_count, block_count), 0
    )
    slots = jnp.sum((same & earlier).astype(jnp.int32), axis=1)
    owner_ids = lax.broadcasted_iota(jnp.int32, (owner_count, slot_count, block_count), 0)
    slot_ids = lax.broadcasted_iota(jnp.int32, (owner_count, slot_count, block_count), 1)
    return ((owners[None, None, :] == owner_ids) & (slots[None, None, :] == slot_ids)).astype(
        jnp.float32
    )


def body(
    grad_parts,
    owners,
    left_stat,
    right_stat,
    left_root,
    right_root,
    first_moment,
    second_moment,
    vec_grad,
    vec_first,
    vec_second,
):
    owner_count = lax.axis_size("mp")
    slot_count, row_count, order = left_stat.shape
    col_count = order // owner_count
    my_rows = lax.axis_index("dp") * row_count
    my_owner = lax.axis_index("mp")
    row_pieces = lax.psum_scatter(
        grad_parts[0].astype(jnp.float32).astype(jnp.bfloat16),
        "dp",
        scatter_dimension=1,
        tiled=True,
    ).astype(jnp.float32)
    selector = owner_table(owners, owner_count, slot_count)
    outgoing = jnp.einsum("ocb,brw->crow", selector, row_pieces, precision=lax.Precision.HIGHEST)
    incoming = lax.all_to_all(
        outgoing.astype(jnp.bfloat16), "mp", split_axis=2, concat_axis=2, tiled=True
    ).astype(outgoing.dtype)
    grad_rows = incoming.reshape(slot_count, row_count, order)
    mine = lax.dynamic_index_in_dim(selector, my_owner, 0, keepdims=False)
    used_mask = (jnp.sum(mine, axis=1) > 0.5)[:, None, None]
    rounded_rows = grad_rows.astype(jnp.bfloat16)
    shard_rows = lax.all_gather(rounded_rows, "dp", axis=1, tiled=True)
    left_part = jnp.einsum(
        "crk,cnk->crn", rounded_rows, shard_rows, preferred_element_type=jnp.float32
    )
    own_cols = lax.dynamic_slice_in_dim(shard_rows, my_rows, row_count, 2)
    right_acc = jnp.einsum("cnr,cnk->crk", own_cols, shard_rows, preferred_element_type=jnp.float32)
    applied_acc = jnp.einsum(
        "crn,cnk->crk", left_root, shard_rows, preferred_element_type=jnp.float32
    )
    scale = 1.0 / order
    left_new = jnp.where(used_mask, left_stat + left_part * scale, left_stat)
    right_new = jnp.where(used_mask, right_stat + right_acc * scale, right_stat)
    first_new = jnp.where(
        used_mask, beta_one * first_moment + (1.0 - beta_one) * grad_rows, first_moment
    )
    second_new = jnp.where(
        used_mask,
        beta_two * second_moment + (1.0 - beta_two) * grad_rows * grad_rows,
        second_moment,
    )
    adam = first_new / (jnp.sqrt(second_new) + adam_eps)
    precond = jnp.einsum(
        "crk,ckm->crm",
        applied_acc.astype(jnp.bfloat16),
        right_root,
        preferred_element_type=jnp.float32,
    )
    square_adam = jnp.sum(adam * adam, axis=(1, 2))
    square_pre = jnp.sum(precond * precond, axis=(1, 2))
    squares = lax.all_gather(jnp.stack([square_adam, square_pre]), "dp")
    square_adam, square_pre = jnp.sum(squares, axis=0)
    vec_all = lax.all_gather(vec_grad[0], "dp")
    vec_sum = jnp.sum(vec_all.astype(jnp.float32), axis=0)
    cells = float(order * order)
    graft = jnp.sqrt(square_adam / cells) / jnp.sqrt(square_pre / cells + graft_eps)
    update_rows = (precond * graft[:, None, None]).astype(jnp.bfloat16)
    returned = lax.all_to_all(
        update_rows.reshape(slot_count, row_count, owner_count, col_count),
        "mp",
        split_axis=2,
        concat_axis=2,
        tiled=True,
    )
    block_update = jnp.einsum(
        "ocb,crow->brw", selector.astype(jnp.bfloat16), returned, preferred_element_type=jnp.float32
    ).astype(jnp.bfloat16)
    vec_first_new = beta_one * vec_first + (1.0 - beta_one) * vec_sum
    vec_second_new = beta_two * vec_second + (1.0 - beta_two) * vec_sum * vec_sum
    vec_update = (vec_first_new / (jnp.sqrt(vec_second_new) + adam_eps)).astype(jnp.bfloat16)
    return (
        block_update,
        left_new,
        right_new,
        first_new,
        second_new,
        vec_update,
        vec_first_new,
        vec_second_new,
    )


def solution(mesh):
    placed = (
        P("dp", None, None, "mp"),
        P(),
        P("mp", "dp", None),
        P("mp", "dp", None),
        P("mp", "dp", None),
        P("mp", None, None),
        P("mp", "dp", None),
        P("mp", "dp", None),
        P("dp", "mp"),
        P("mp"),
        P("mp"),
    )
    return jax.shard_map(
        body,
        mesh=mesh,
        in_specs=placed,
        out_specs=(
            P(None, "dp", "mp"),
            P("mp", "dp", None),
            P("mp", "dp", None),
            P("mp", "dp", None),
            P("mp", "dp", None),
            P("mp"),
            P("mp"),
            P("mp"),
        ),
        check_vma=False,
    )
```

```python
import heapq

import jax
import jax.numpy as jnp
from jax import lax
from jax.experimental import pallas as pl
from jax.experimental.pallas import tpu as pltpu
from jax.sharding import PartitionSpec as P

beta_one = 0.9
beta_two = 0.95
adam_eps = 1e-08
graft_eps = 1e-06

MESH = pl.DeviceIdType.MESH
NX, NZ, NY, NC = 4, 8, 4, 2
N_MP = NY * NC
BLOCKS, SLOT_COUNT, ROWS, ORDER, COLS = 16, 4, 32, 1024, 128
HALF = ROWS // NC
N_SEMS = 224
bf16, f32 = jnp.bfloat16, jnp.float32


def kernel(
    owners, grad, lroot, rroot, lstat, rstat, mom1, mom2, vecg,
    upd_out, left_out, right_out, first_out, second_out, vec_out,
    gin, rbz1, rbz2, ra1, rr1, rs1, ra2, rr2, rs2, r1, r2, fin, gfull,
    ly, lsel, lhome, lhs1, lhs2, res, held0, held1, held2, held3, stage, won, rrv, lsv, rsv, m1v, m2v,
    out_l, out_r, out_1, out_2, prec, upd_in, norm_me, norm_z, norm_x, norm_m, vx, vs, vz, upd_s,
    send_sems, recv_sems, local_sems,
):
    dp, mp = lax.axis_index("dp"), lax.axis_index("mp")
    x, z = dp // NZ, lax.rem(dp, NZ)
    y, c = mp // NC, lax.rem(mp, NC)
    held = (held0, held1, held2, held3)
    counts = {"remote": 0, "local": 0}
    sent = []

    def xdev(k):
        return (lax.rem(x + k + NX, NX) * NZ + z, mp)

    def zdev(k):
        return (x * NZ + lax.rem(z + k + NZ, NZ), mp)

    def ydev(k):
        return (dp, lax.rem(y + k + NY, NY) * NC + c)

    sibling = (dp, y * NC + 1 - c)

    def send(src, dst, device):
        i = counts["remote"]
        counts["remote"] += 1
        copy = pltpu.make_async_remote_copy(
            src_ref=src, dst_ref=dst, send_sem=send_sems.at[i], recv_sem=recv_sems.at[i],
            device_id=device, device_id_type=MESH,
        )
        copy.start()
        sent.append(copy)
        return copy

    def local(src, dst):
        i = counts["local"]
        counts["local"] += 1
        copy = pltpu.make_async_copy(src, dst, local_sems.at[i])
        copy.start()
        return copy

    load_z = local(grad.at[:, 2:4], gin.at[:, 2:4])
    load_x = local(grad.at[:, 0:2], gin.at[:, 0:2])
    load_l = local(lroot.at[:, c], ly.at[y, c])

    barrier = pltpu.get_barrier_semaphore()
    partners = [xdev(k) for k in range(1, NX)] + [zdev(k) for k in range(1, NZ)]
    partners += [(dp, lax.rem(mp + k, N_MP)) for k in range(1, N_MP)]
    for device in partners:
        pl.semaphore_signal(barrier, inc=1, device_id=device, device_id_type=MESH)

    load_r = local(rroot, rrv)
    load_1 = local(mom1, m1v)
    load_2 = local(mom2, m2v)
    load_ls = local(lstat, lsv)
    load_rs = local(rstat, rsv)

    own = [owners[b] for b in range(BLOCKS)]
    slot = []
    for b in range(BLOCKS):
        s = 0
        for a in range(b):
            s = s + jnp.where(own[a] == own[b], 1, 0)
        slot.append(s)
    place = [0] + [jnp.minimum(s, SLOT_COUNT - 1) for s in slot[1:]]

    def picks(who):
        chosen = []
        for s in range(SLOT_COUNT):
            p = jnp.int32(0)
            for b in range(BLOCKS):
                p = p + jnp.where((own[b] == who) & (slot[b] == s), b, 0)
            chosen.append(p)
        return chosen

    mine, theirs = picks(mp), picks(y * NC + 1 - c)
    owned = jnp.int32(0)
    for b in range(BLOCKS):
        owned = owned + jnp.where(own[b] == mp, 1, 0)

    load_z.wait()
    load_x.wait()
    pl.semaphore_wait(barrier, len(partners))

    def accumulate(into, term):
        into[...] = into[...] + term[...]

    queue = []
    clock = {"t": 0.0, "n": 0}
    done = set()

    def spawn(gen, t):
        clock["n"] += 1
        heapq.heappush(queue, (t, clock["n"], gen))

    def run():
        while queue:
            t, _, gen = heapq.heappop(queue)
            clock["t"] = t
            try:
                nxt = next(gen)
            except StopIteration:
                continue
            spawn(gen, nxt)

    def need(*names):
        while not all(n in done for n in names):
            yield clock["t"] + 0.25

    def z_stream(name, d, h, term, rb, t0, dt):
        steps = 4 if (h == 0) == (d == 1) else 3
        di = 0 if d == 1 else 1
        copy = send(term(lax.rem(z + d * steps + NZ, NZ), h), rb.at[di, h, 0], zdev(d))
        for s in range(steps):
            yield t0 + (s + 1) * dt
            copy.wait_recv()
            if s < steps - 1:
                accumulate(rb.at[di, h, s], term(lax.rem(z + d * (steps - 1 - s) + NZ, NZ), h))
                copy = send(rb.at[di, h, s], rb.at[di, h, s + 1], zdev(d))
        done.add((name, d, h))

    def last(d, h):
        return 3 if (h == 0) == (d == 1) else 2

    def x_stream(name, term, ra, rr, rs, put, times):
        first, raw, second = {}, {}, {}
        for d, di in ((1, 0), (-1, 1)):
            first[d] = send(term(lax.rem(x + 2, NX), di), ra.at[di], xdev(d))
        yield times[0]
        for d, di in ((1, 0), (-1, 1)):
            raw[d] = send(term(lax.rem(x + d + NX, NX), 1 - di), rr.at[di], xdev(d))
        yield times[1]
        for d, di in ((1, 0), (-1, 1)):
            first[d].wait_recv()
            accumulate(ra.at[di], term(lax.rem(x + d + NX, NX), di))
            second[d] = send(ra.at[di], rs.at[di], xdev(d))
        yield times[2]
        for d in (1, -1):
            raw[d].wait_recv()
            second[d].wait_recv()
        put(0, add3(term(x, 0), rs.at[0], rr.at[1]))
        put(1, add3(term(x, 1), rr.at[0], rs.at[1]))
        done.add(name)

    def add3(a, b, d):
        return (a[...].astype(f32) + b[...].astype(f32) + d[...].astype(f32)).astype(bf16)

    def term_z1(Z, h):
        return gin.at[2 * h : 2 * h + 2, 2:4, :, Z]

    for d, h in ((1, 0), (-1, 1), (1, 1), (-1, 0)):
        spawn(z_stream("z1", d, h, term_z1, rbz1, 0.5 + 2.8 * ((h == 0) != (d == 1)), 5.6), 0)

    def x_stage_one(yb):
        def term(X, h):
            return gin.at[X, yb, 2 * h : 2 * h + 2]

        def put(h, value):
            r1[yb, 2 * h : 2 * h + 2] = value

        t = 2.8 * yb
        return x_stream(("x1", yb), term, ra1.at[yb], rr1.at[yb], rs1.at[yb], put, (0.1 + yb / 100, 4.6 + t, 16.4 + t))

    for yb in range(2):
        spawn(x_stage_one(yb), 0)

    def z_stage_two(yb):
        yield 16.0
        yield from need(("x1", yb))
        t = clock["t"]

        def term(Z, h):
            return r1.at[h, :, Z]

        for d in (1, -1):
            spawn(z_stream("z2", d, yb, term, rbz2, t, 2.4), t)
        yield t + 0.1
        yield from need(("z2", 1, yb), ("z2", -1, yb))
        fin[yb] = add3(r1.at[yb, :, z], rbz2.at[0, yb, last(1, yb)], rbz2.at[1, yb, last(-1, yb)])
        done.add(("fin", yb))

    for yb in range(2):
        spawn(z_stage_two(yb), 1)

    def x_stage_two():
        yield 20.0
        for h in (0, 1):
            yield from need(("z1", 1, h), ("z1", -1, h))
            r2[2 * h : 2 * h + 2] = add3(
                gin.at[2 * h : 2 * h + 2, 2:4, :, z], rbz1.at[0, h, last(1, h)], rbz1.at[1, h, last(-1, h)]
            )

        def term(X, h):
            return r2.at[X, h]

        def put(h, value):
            fin[2 + h] = value

        t = clock["t"]
        yield from x_stream("x2", term, ra2, rr2, rs2, put, (t, t + 2.4, t + 4.8))

    spawn(x_stage_two(), 1)

    def left_roots():
        got = send(lroot.at[:, 1 - c], ly.at[y, c], sibling)
        yield 3.0
        load_l.wait()
        got.wait_recv()
        copies = {}
        for d in (1, -1):
            copies[d] = send(ly.at[y], ly.at[y], ydev(d))
        yield 12.0
        relays = []
        for d, oc in ((1, 0), (-1, 1)):
            copies[d].wait_recv()
            frm = lax.rem(y - d + NY, NY)
            relays.append(send(ly.at[frm, oc], ly.at[frm, oc], ydev(d)))
        yield 18.5
        for copy in relays:
            copy.wait_recv()
        for xb in range(NX):
            o, s = jnp.int32(0), jnp.int32(0)
            for yb in range(NY):
                o = o + jnp.where(y == yb, own[NY * xb + yb], 0)
                s = s + jnp.where(y == yb, place[NY * xb + yb], 0)
            lsel[xb] = ly[o // NC, lax.rem(o, NC), s]
        copies = []
        for k in range(1, NX):
            copies.append(send(lsel.at[lax.rem(x + k, NX)], lhome.at[x], xdev(k)))
        lhome[x] = lsel[x]
        yield 26.0
        for copy in copies:
            copy.wait_recv()
        lhs2[0 : NX * HALF] = lhome[...].reshape(NX * HALF, ORDER)
        done.add("left_roots")

    spawn(left_roots(), 0.6)

    def deliver(t, src, t0, hop):
        copies = []
        for k in range(1, NX):
            copies.append(send(src(lax.rem(x + k, NX)), held[t].at[y, x], xdev(k)))
        keep = local(src(x), held[t].at[y, x])
        yield t0 + hop
        keep.wait()
        for copy in copies:
            copy.wait_recv()
        copies = {}
        for d in (1, -1):
            copies[d] = send(held[t].at[y], held[t].at[y], ydev(d))
        yield t0 + 2.5 * hop
        relays = []
        for d, hb in ((1, 0), (-1, 1)):
            copies[d].wait_recv()
            frm = lax.rem(y - d + NY, NY)
            part = held[t].at[frm, 2 * hb : 2 * hb + 2]
            relays.append(send(part, part, ydev(d)))
        yield t0 + 3.5 * hop
        for copy in relays:
            copy.wait_recv()
        for s in range(SLOT_COUNT):
            b = theirs[s]
            stage[t, s] = held[t][lax.rem(b, NY), b // NY]
        got = send(stage.at[t], won.at[t, :, c], sibling)
        for s in range(SLOT_COUNT):
            b = mine[s]
            won[t, s, c] = held[t][lax.rem(b, NY), b // NY]
        yield t0 + 4 * hop
        got.wait_recv()
        done.add(("won", t))

    def used(s):
        return jnp.full((ROWS, ORDER), owned, jnp.int32) > s

    def row(s):
        return lax.broadcasted_iota(jnp.int32, (8, COLS), 0) == s

    def slot_rows(t, s):
        return won[t, s].reshape(ROWS, ORDER).astype(f32)

    norm_tile = {"v": jnp.zeros((8, COLS), f32)}
    stores = []

    def moments(t0):
        yield from need(("won", 0))
        load_1.wait()
        load_2.wait()
        for s in range(SLOT_COUNT):
            g = slot_rows(0, s)
            m1, m2 = m1v[s], m2v[s]
            n1 = jnp.where(used(s), beta_one * m1 + (1.0 - beta_one) * g, m1)
            n2 = jnp.where(used(s), beta_two * m2 + (1.0 - beta_two) * g * g, m2)
            out_1[s] = n1
            out_2[s] = n2
            adam = n1 / (jnp.sqrt(n2) + adam_eps)
            norm_tile["v"] = jnp.where(row(s), jnp.sum(adam * adam), norm_tile["v"])
        stores.append(local(out_1, first_out))
        stores.append(local(out_2, second_out))
        done.add("moments")

    def statistics(t, load, stat, out, dst):
        yield from need(("won", t))
        load.wait()
        for s in range(SLOT_COUNT):
            old = stat[s]
            out[s] = jnp.where(used(s), old + slot_rows(t, s) * (1.0 / ORDER), old)
        stores.append(local(out, dst))

    def vectors():
        copies = [send(vecg, vx.at[k - 1], xdev(k)) for k in range(1, NX)]
        yield 15.0
        for copy in copies:
            copy.wait_recv()
        vs[...] = vecg[...] + vx[0] + vx[1] + vx[2]
        yield 48.0
        yield from need("gathered")
        copies = [send(vs, vz.at[k - 1], zdev(k)) for k in range(1, NZ)]
        yield clock["t"] + 12.0
        total = vs[...]
        for k, copy in enumerate(copies):
            copy.wait_recv()
            total = total + vz[k]
        vec_out[...] = total

    spawn(vectors(), 0.7)

    def main():
        yield 22.0
        yield from need(("fin", 0), ("fin", 1), "x2")
        copies = []
        for k in range(1, N_MP):
            to = lax.rem(mp + k, N_MP)
            yt, ct = to // NC, lax.rem(to, NC)
            copies.append(
                send(
                    fin.at[yt, :, pl.ds(pl.multiple_of(ct * HALF, HALF), HALF)],
                    gfull.at[:, z, ct, :, pl.ds(pl.multiple_of(mp * COLS, COLS), COLS)],
                    (dp, to),
                )
            )
        keep = local(
            fin.at[y, :, pl.ds(pl.multiple_of(c * HALF, HALF), HALF)],
            gfull.at[:, z, c, :, pl.ds(pl.multiple_of(mp * COLS, COLS), COLS)],
        )
        t = clock["t"] + 3.5
        yield t
        keep.wait()
        for copy in copies:
            copy.wait_recv()

        over, ring = [], {}

        def chunk(h, src):
            return gfull.at[2 * h : 2 * h + 2, src, c]

        for h in (0, 1):
            for d in (1, -1):
                ring[d, h] = send(chunk(h, z), chunk(h, z), zdev(d))
        over.append(send(gfull.at[:, z, c], gfull.at[:, z, c], sibling))
        spawn(deliver(0, lambda xt: gfull.at[xt, z, c], t, 3.0), t)
        spawn(moments(t), t + 8)
        for s in range(4):
            for h in (0, 1):
                yield t + (s + 1) * 3.0 + h * 1.5
                for d in (1, -1):
                    if (d, h) not in ring:
                        continue
                    ring.pop((d, h)).wait_recv()
                    src = lax.rem(z - d * (s + 1) + NZ, NZ)
                    if s < 2 or (s == 2 and (h == 0) == (d == 1)):
                        ring[d, h] = send(chunk(h, src), chunk(h, src), zdev(d))
                    over.append(send(chunk(h, src), chunk(h, src), sibling))
        done.add("gathered")

        rows_of = NX * HALF
        i = lax.broadcasted_iota(jnp.int32, (rows_of, ORDER), 0)
        j = lax.broadcasted_iota(jnp.int32, (rows_of, ORDER), 1)
        wanted = (i // HALF) * (NZ * ROWS) + z * ROWS + c * HALF + lax.rem(i, HALF)
        lhs1[rows_of:] = jnp.where(j == wanted, 1.0, 0.0).astype(bf16)
        lhs1[0:rows_of] = gfull[:, z, c].reshape(rows_of, ORDER)
        for copy in over:
            copy.wait_recv()
        width = NZ * ROWS
        for n in range(NX):
            o = lax.dot_general(
                lhs1[...], gfull[n].reshape(width, ORDER), (((1,), (1,)), ((), ())), preferred_element_type=f32
            )
            res[1, :, :, n * width : (n + 1) * width] = o[0:rows_of].reshape(NX, HALF, width).astype(bf16)
            lhs2[rows_of:, n * width : (n + 1) * width] = o[rows_of:].astype(bf16)
        yield from need("left_roots")
        for n in range(NX):
            o = jnp.dot(
                lhs2[...],
                gfull[:, :, :, :, n * width : (n + 1) * width].reshape(ORDER, width),
                preferred_element_type=f32,
            )
            res[0, :, :, n * width : (n + 1) * width] = o[0:rows_of].reshape(NX, HALF, width).astype(bf16)
            res[2, :, :, n * width : (n + 1) * width] = o[rows_of:].reshape(NX, HALF, width).astype(bf16)
        t = clock["t"] + 3.0
        for r in range(3):
            spawn(deliver(1 + r, lambda xt, r=r: res.at[r, xt], t + 2.0 * r, 3.0), t + 0.01 * r)
        spawn(statistics(2, load_ls, lsv, out_l, left_out), t + 14)
        spawn(statistics(3, load_rs, rsv, out_r, right_out), t + 16)
        yield t + 10
        yield from need(("won", 1), "moments")
        load_r.wait()
        tile = norm_tile["v"]
        for s in range(SLOT_COUNT):
            p = jnp.dot(won[1, s].reshape(ROWS, ORDER), rrv[s], preferred_element_type=f32)
            prec[s] = p.astype(bf16)
            tile = jnp.where(row(SLOT_COUNT + s), jnp.sum(p * p), tile)
        norm_me[...] = tile
        copies_n = [send(norm_me, norm_z.at[k - 1], zdev(k)) for k in range(1, NZ)]
        copies_u = []
        for k in range(1, N_MP):
            to = lax.rem(mp + k, N_MP)
            cols = pl.ds(pl.multiple_of(to * COLS, COLS), COLS)
            copies_u.append(send(prec.at[:, :, cols], upd_in.at[mp], (dp, to)))
        keep = local(prec.at[:, :, pl.ds(pl.multiple_of(mp * COLS, COLS), COLS)], upd_in.at[mp])
        yield clock["t"] + 4.0
        for k, copy in enumerate(copies_n):
            copy.wait_recv()
            tile = tile + norm_z[k]
        norm_me2 = norm_x.at[NX - 1]
        norm_me2[...] = tile
        copies_n = [send(norm_me2, norm_x.at[k - 1], xdev(k)) for k in range(1, NX)]
        yield clock["t"] + 3.0
        for k, copy in enumerate(copies_n):
            copy.wait_recv()
            tile = tile + norm_x[k]
        cells = float(ORDER * ORDER)
        graft = jnp.sqrt(tile[0:SLOT_COUNT] / cells) / jnp.sqrt(tile[SLOT_COUNT:] / cells + graft_eps)
        norm_m[mp] = jnp.concatenate([graft, graft], axis=0)
        copies_n = [send(norm_m.at[mp], norm_m.at[mp], (dp, lax.rem(mp + k, N_MP))) for k in range(1, N_MP)]
        yield clock["t"] + 3.0
        keep.wait()
        for copy in copies_u + copies_n:
            copy.wait_recv()
        for b in range(BLOCKS):
            g = jnp.sum(jnp.where(row(place[b]), norm_m[own[b]], 0.0), axis=0, keepdims=True)
            upd_s[b] = (upd_in[own[b], place[b]].astype(f32) * g).astype(bf16)
        stores.append(local(upd_s, upd_out))

    spawn(main(), 2)
    run()
    for copy in stores:
        copy.wait()
    for copy in sent:
        copy.wait_send()
    assert counts["remote"] <= N_SEMS, counts


def body(
    grad_parts, owners, left_stat, right_stat, left_root, right_root, first_moment, second_moment,
    vec_grad, vec_first, vec_second,
):
    hbm = pl.BlockSpec(memory_space=pl.ANY)
    vmem = pl.BlockSpec(memory_space=pltpu.VMEM)
    smem = pl.BlockSpec(memory_space=pltpu.SMEM)
    slots = jax.ShapeDtypeStruct((SLOT_COUNT, ROWS, ORDER), f32)
    vec_rows = vec_grad.shape[1] // COLS
    V = pltpu.VMEM
    scratch = [
        V((NX, NY, NX, NZ, ROWS, COLS), bf16),
        V((2, 2, 4, 2, 2, NX, ROWS, COLS), bf16),
        V((2, 2, 4, NX, ROWS, COLS), bf16),
        V((2, 2, 2, NZ, ROWS, COLS), bf16),
        V((2, 2, 2, NZ, ROWS, COLS), bf16),
        V((2, 2, 2, NZ, ROWS, COLS), bf16),
        V((2, NX, ROWS, COLS), bf16),
        V((2, NX, ROWS, COLS), bf16),
        V((2, NX, ROWS, COLS), bf16),
        V((2, NX, NZ, ROWS, COLS), bf16),
        V((NX, 2, NX, ROWS, COLS), bf16),
        V((NY, NX, ROWS, COLS), bf16),
        V((NX, NZ, NC, HALF, ORDER), bf16),
        V((NY, NC, SLOT_COUNT, HALF, ORDER), bf16),
        V((NX, HALF, ORDER), bf16),
        V((NX, HALF, ORDER), bf16),
        V((2 * NX * HALF, ORDER), bf16),
        V((2 * NX * HALF, ORDER), bf16),
        V((3, NX, HALF, ORDER), bf16),
        *[V((NY, NX, HALF, ORDER), bf16)] * 4,
        V((4, SLOT_COUNT, HALF, ORDER), bf16),
        V((4, SLOT_COUNT, NC, HALF, ORDER), bf16),
        V((SLOT_COUNT, ORDER, ORDER), bf16),
        V((SLOT_COUNT, ROWS, ORDER), f32),
        V((SLOT_COUNT, ROWS, ORDER), f32),
        V((SLOT_COUNT, ROWS, ORDER), f32),
        V((SLOT_COUNT, ROWS, ORDER), f32),
        V((SLOT_COUNT, ROWS, ORDER), f32),
        V((SLOT_COUNT, ROWS, ORDER), f32),
        V((SLOT_COUNT, ROWS, ORDER), f32),
        V((SLOT_COUNT, ROWS, ORDER), f32),
        V((SLOT_COUNT, ROWS, ORDER), bf16),
        V((N_MP, SLOT_COUNT, ROWS, COLS), bf16),
        V((8, COLS), f32),
        V((NZ - 1, 8, COLS), f32),
        V((NX, 8, COLS), f32),
        V((N_MP, 8, COLS), f32),
        V((NX - 1, vec_rows, COLS), f32),
        V((vec_rows, COLS), f32),
        V((NZ - 1, vec_rows, COLS), f32),
        V((BLOCKS, ROWS, COLS), bf16),
        pltpu.SemaphoreType.DMA((N_SEMS,)),
        pltpu.SemaphoreType.DMA((N_SEMS,)),
        pltpu.SemaphoreType.DMA((24,)),
    ]
    block_update, left_new, right_new, first_new, second_new, vec_sum = pl.pallas_call(
        kernel,
        out_shape=(
            jax.ShapeDtypeStruct((BLOCKS, ROWS, COLS), bf16), slots, slots, slots, slots,
            jax.ShapeDtypeStruct((vec_rows, COLS), f32),
        ),
        in_specs=[smem] + [hbm] * 7 + [vmem],
        out_specs=(hbm,) * 5 + (vmem,),
        scratch_shapes=scratch,
        compiler_params=pltpu.CompilerParams(
            collective_id=0, has_side_effects=True, vmem_limit_bytes=62 * 1024 * 1024
        ),
    )(
        owners,
        grad_parts.reshape(NX, NY, NX, NZ, ROWS, COLS),
        left_root.reshape(SLOT_COUNT, NC, HALF, ORDER),
        right_root,
        left_stat,
        right_stat,
        first_moment,
        second_moment,
        vec_grad.astype(f32).reshape(vec_rows, COLS),
    )
    vec_sum = vec_sum.reshape(vec_first.shape)
    vec_first_new = beta_one * vec_first + (1.0 - beta_one) * vec_sum
    vec_second_new = beta_two * vec_second + (1.0 - beta_two) * vec_sum * vec_sum
    vec_update = (vec_first_new / (jnp.sqrt(vec_second_new) + adam_eps)).astype(bf16)
    return (
        block_update,
        left_new,
        right_new,
        first_new,
        second_new,
        vec_update,
        vec_first_new,
        vec_second_new,
    )


def solution(mesh):
    slots = P("mp", "dp", None)
    return jax.shard_map(
        body,
        mesh=mesh,
        in_specs=(
            P("dp", None, None, "mp"), P(), slots, slots, slots, P("mp", None, None), slots, slots,
            P("dp", "mp"), P("mp"), P("mp"),
        ),
        out_specs=(P(None, "dp", "mp"), slots, slots, slots, slots, P("mp"), P("mp"), P("mp")),
        check_vma=False,
    )
```

```python
import heapq

import jax
import jax.numpy as jnp
from jax import lax
from jax.experimental import pallas as pl
from jax.experimental.pallas import tpu as pltpu
from jax.sharding import PartitionSpec as P

beta_one = 0.9
beta_two = 0.95
adam_eps = 1e-08
graft_eps = 1e-06

MESH = pl.DeviceIdType.MESH
NX, NZ, NY, NC = 4, 8, 4, 2
N_MP = NY * NC
BLOCKS, SLOT_COUNT, ROWS, ORDER, COLS = 16, 4, 32, 1024, 128
HALF = ROWS // NC
N_SEMS = 224
bf16, f32 = jnp.bfloat16, jnp.float32


def kernel(
    owners, grad, lroot, rroot, lstat, rstat, mom1, mom2, vecg,
    upd_out, left_out, right_out, first_out, second_out, vec_out,
    gin, rbz1, rbz2, ra1, rr1, rs1, ra2, rr2, rs2, r1, r2, fin, gfull,
    ly, lsel, lhome, lhs1, lhs2, res, held0, held1, held2, held3, stage, won, rrv, lsv, rsv, m1v, m2v,
    out_l, out_r, out_1, out_2, prec, upd_in, norm_me, norm_z, norm_x, norm_m, vx, vs, vz, upd_s,
    send_sems, recv_sems, local_sems,
):
    dp, mp = lax.axis_index("dp"), lax.axis_index("mp")
    x, z = dp // NZ, lax.rem(dp, NZ)
    y, c = mp // NC, lax.rem(mp, NC)
    held = (held0, held1, held2, held3)
    counts = {"remote": 0, "local": 0}
    sent = []

    def xdev(k):
        return (lax.rem(x + k + NX, NX) * NZ + z, mp)

    def zdev(k):
        return (x * NZ + lax.rem(z + k + NZ, NZ), mp)

    def ydev(k):
        return (dp, lax.rem(y + k + NY, NY) * NC + c)

    sibling = (dp, y * NC + 1 - c)

    def send(src, dst, device):
        i = counts["remote"]
        counts["remote"] += 1
        copy = pltpu.make_async_remote_copy(
            src_ref=src, dst_ref=dst, send_sem=send_sems.at[i], recv_sem=recv_sems.at[i],
            device_id=device, device_id_type=MESH,
        )
        copy.start()
        sent.append(copy)
        return copy

    def local(src, dst):
        i = counts["local"]
        counts["local"] += 1
        copy = pltpu.make_async_copy(src, dst, local_sems.at[i])
        copy.start()
        return copy

    load_z = local(grad.at[:, 2:4], gin.at[:, 2:4])
    load_x = local(grad.at[:, 0:2], gin.at[:, 0:2])
    load_l = local(lroot.at[:, c], ly.at[y, c])

    barrier = pltpu.get_barrier_semaphore()
    partners = [xdev(k) for k in range(1, NX)] + [zdev(k) for k in range(1, NZ)]
    partners += [(dp, lax.rem(mp + k, N_MP)) for k in range(1, N_MP)]
    for device in partners:
        pl.semaphore_signal(barrier, inc=1, device_id=device, device_id_type=MESH)

    load_r = local(rroot, rrv)
    load_1 = local(mom1, m1v)
    load_2 = local(mom2, m2v)
    load_ls = local(lstat, lsv)
    load_rs = local(rstat, rsv)

    own = [owners[b] for b in range(BLOCKS)]
    slot = []
    for b in range(BLOCKS):
        s = 0
        for a in range(b):
            s = s + jnp.where(own[a] == own[b], 1, 0)
        slot.append(s)
    place = [0] + [jnp.minimum(s, SLOT_COUNT - 1) for s in slot[1:]]

    def picks(who):
        chosen = []
        for s in range(SLOT_COUNT):
            p = jnp.int32(0)
            for b in range(BLOCKS):
                p = p + jnp.where((own[b] == who) & (slot[b] == s), b, 0)
            chosen.append(p)
        return chosen

    mine, theirs = picks(mp), picks(y * NC + 1 - c)
    owned = jnp.int32(0)
    for b in range(BLOCKS):
        owned = owned + jnp.where(own[b] == mp, 1, 0)

    load_z.wait()
    load_x.wait()
    pl.semaphore_wait(barrier, len(partners))

    def accumulate(into, term):
        into[...] = into[...] + term[...]

    queue = []
    clock = {"t": 0.0, "n": 0}
    done = set()

    def spawn(gen, t):
        clock["n"] += 1
        heapq.heappush(queue, (t, clock["n"], gen))

    def run():
        while queue:
            t, _, gen = heapq.heappop(queue)
            clock["t"] = t
            try:
                nxt = next(gen)
            except StopIteration:
                continue
            spawn(gen, nxt)

    def need(*names):
        while not all(n in done for n in names):
            yield clock["t"] + 0.25

    def z_stream(name, d, h, term, rb, t0, dt):
        steps = 4 if (h == 0) == (d == 1) else 3
        di = 0 if d == 1 else 1
        copy = send(term(lax.rem(z + d * steps + NZ, NZ), h), rb.at[di, h, 0], zdev(d))
        for s in range(steps):
            yield t0 + (s + 1) * dt
            copy.wait_recv()
            if s < steps - 1:
                accumulate(rb.at[di, h, s], term(lax.rem(z + d * (steps - 1 - s) + NZ, NZ), h))
                copy = send(rb.at[di, h, s], rb.at[di, h, s + 1], zdev(d))
        done.add((name, d, h))

    def last(d, h):
        return 3 if (h == 0) == (d == 1) else 2

    def x_stream(name, term, ra, rr, rs, put, times):
        first, raw, second = {}, {}, {}
        for d, di in ((1, 0), (-1, 1)):
            first[d] = send(term(lax.rem(x + 2, NX), di), ra.at[di], xdev(d))
        yield times[0]
        for d, di in ((1, 0), (-1, 1)):
            raw[d] = send(term(lax.rem(x + d + NX, NX), 1 - di), rr.at[di], xdev(d))
        yield times[1]
        for d, di in ((1, 0), (-1, 1)):
            first[d].wait_recv()
            accumulate(ra.at[di], term(lax.rem(x + d + NX, NX), di))
            second[d] = send(ra.at[di], rs.at[di], xdev(d))
        yield times[2]
        for d in (1, -1):
            raw[d].wait_recv()
            second[d].wait_recv()
        put(0, add3(term(x, 0), rs.at[0], rr.at[1]))
        put(1, add3(term(x, 1), rr.at[0], rs.at[1]))
        done.add(name)

    def add3(a, b, d):
        return (a[...].astype(f32) + b[...].astype(f32) + d[...].astype(f32)).astype(bf16)

    def term_z1(Z, h):
        return gin.at[2 * h : 2 * h + 2, 2:4, :, Z]

    for d, h in ((1, 0), (-1, 1), (1, 1), (-1, 0)):
        spawn(z_stream("z1", d, h, term_z1, rbz1, 0.5 + 2.8 * ((h == 0) != (d == 1)), 5.6), 0)

    def x_stage_one(yb):
        def term(X, h):
            return gin.at[X, yb, 2 * h : 2 * h + 2]

        def put(h, value):
            r1[yb, 2 * h : 2 * h + 2] = value

        t = 2.8 * yb
        return x_stream(("x1", yb), term, ra1.at[yb], rr1.at[yb], rs1.at[yb], put, (0.1 + yb / 100, 4.6 + t, 16.4 + t))

    for yb in range(2):
        spawn(x_stage_one(yb), 0)

    def z_stage_two(yb):
        yield 16.0
        yield from need(("x1", yb))
        t = clock["t"]

        def term(Z, h):
            return r1.at[h, :, Z]

        for d in (1, -1):
            spawn(z_stream("z2", d, yb, term, rbz2, t, 2.4), t)
        yield t + 0.1
        yield from need(("z2", 1, yb), ("z2", -1, yb))
        fin[yb] = add3(r1.at[yb, :, z], rbz2.at[0, yb, last(1, yb)], rbz2.at[1, yb, last(-1, yb)])
        done.add(("fin", yb))

    for yb in range(2):
        spawn(z_stage_two(yb), 1)

    def x_stage_two():
        yield 20.0
        for h in (0, 1):
            yield from need(("z1", 1, h), ("z1", -1, h))
            r2[2 * h : 2 * h + 2] = add3(
                gin.at[2 * h : 2 * h + 2, 2:4, :, z], rbz1.at[0, h, last(1, h)], rbz1.at[1, h, last(-1, h)]
            )

        def term(X, h):
            return r2.at[X, h]

        def put(h, value):
            fin[2 + h] = value

        t = clock["t"]
        yield from x_stream("x2", term, ra2, rr2, rs2, put, (t, t + 2.4, t + 4.8))

    spawn(x_stage_two(), 1)

    def left_roots():
        got = send(lroot.at[:, 1 - c], ly.at[y, c], sibling)
        yield 3.0
        load_l.wait()
        got.wait_recv()
        copies = {}
        for d in (1, -1):
            copies[d] = send(ly.at[y], ly.at[y], ydev(d))
        yield 12.0
        relays = []
        for d, oc in ((1, 0), (-1, 1)):
            copies[d].wait_recv()
            frm = lax.rem(y - d + NY, NY)
            relays.append(send(ly.at[frm, oc], ly.at[frm, oc], ydev(d)))
        yield 18.5
        for copy in relays:
            copy.wait_recv()
        for xb in range(NX):
            o, s = jnp.int32(0), jnp.int32(0)
            for yb in range(NY):
                o = o + jnp.where(y == yb, own[NY * xb + yb], 0)
                s = s + jnp.where(y == yb, place[NY * xb + yb], 0)
            lsel[xb] = ly[o // NC, lax.rem(o, NC), s]
        copies = []
        for k in range(1, NX):
            copies.append(send(lsel.at[lax.rem(x + k, NX)], lhome.at[x], xdev(k)))
        lhome[x] = lsel[x]
        yield 26.0
        for copy in copies:
            copy.wait_recv()
        lhs2[0 : NX * HALF] = lhome[...].reshape(NX * HALF, ORDER)
        done.add("left_roots")

    spawn(left_roots(), 0.6)

    def deliver(t, src, t0, hop):
        copies = []
        for k in range(1, NX):
            copies.append(send(src(lax.rem(x + k, NX)), held[t].at[y, x], xdev(k)))
        keep = local(src(x), held[t].at[y, x])
        yield t0 + hop
        keep.wait()
        for copy in copies:
            copy.wait_recv()
        copies = {}
        for d in (1, -1):
            copies[d] = send(held[t].at[y], held[t].at[y], ydev(d))
        yield t0 + 2.5 * hop
        relays = []
        for d, hb in ((1, 0), (-1, 1)):
            copies[d].wait_recv()
            frm = lax.rem(y - d + NY, NY)
            part = held[t].at[frm, 2 * hb : 2 * hb + 2]
            relays.append(send(part, part, ydev(d)))
        yield t0 + 3.5 * hop
        for copy in relays:
            copy.wait_recv()
        for s in range(SLOT_COUNT):
            b = theirs[s]
            stage[t, s] = held[t][lax.rem(b, NY), b // NY]
        got = send(stage.at[t], won.at[t, :, c], sibling)
        for s in range(SLOT_COUNT):
            b = mine[s]
            won[t, s, c] = held[t][lax.rem(b, NY), b // NY]
        yield t0 + 4 * hop
        got.wait_recv()
        done.add(("won", t))

    def used(s):
        return jnp.full((ROWS, ORDER), owned, jnp.int32) > s

    def row(s):
        return lax.broadcasted_iota(jnp.int32, (8, COLS), 0) == s

    def slot_rows(t, s):
        return won[t, s].reshape(ROWS, ORDER).astype(f32)

    norm_tile = {"v": jnp.zeros((8, COLS), f32)}
    stores = []

    def moments(t0):
        yield from need(("won", 0))
        load_1.wait()
        load_2.wait()
        for s in range(SLOT_COUNT):
            g = slot_rows(0, s)
            m1, m2 = m1v[s], m2v[s]
            n1 = jnp.where(used(s), beta_one * m1 + (1.0 - beta_one) * g, m1)
            n2 = jnp.where(used(s), beta_two * m2 + (1.0 - beta_two) * g * g, m2)
            out_1[s] = n1
            out_2[s] = n2
            adam = n1 / (jnp.sqrt(n2) + adam_eps)
            norm_tile["v"] = jnp.where(row(s), jnp.sum(adam * adam), norm_tile["v"])
        stores.append(local(out_1, first_out))
        stores.append(local(out_2, second_out))
        done.add("moments")

    def statistics(t, load, stat, out, dst):
        yield from need(("won", t))
        load.wait()
        for s in range(SLOT_COUNT):
            old = stat[s]
            out[s] = jnp.where(used(s), old + slot_rows(t, s) * (1.0 / ORDER), old)
        stores.append(local(out, dst))

    def vectors():
        copies = [send(vecg, vx.at[k - 1], xdev(k)) for k in range(1, NX)]
        yield 15.0
        for copy in copies:
            copy.wait_recv()
        vs[...] = vecg[...] + vx[0] + vx[1] + vx[2]
        yield 48.0
        yield from need("gathered")
        copies = [send(vs, vz.at[k - 1], zdev(k)) for k in range(1, NZ)]
        yield clock["t"] + 12.0
        total = vs[...]
        for k, copy in enumerate(copies):
            copy.wait_recv()
            total = total + vz[k]
        vec_out[...] = total

    spawn(vectors(), 0.7)

    def main():
        yield 22.0
        yield from need(("fin", 0), ("fin", 1), "x2")
        copies = []
        for k in range(1, N_MP):
            to = lax.rem(mp + k, N_MP)
            yt, ct = to // NC, lax.rem(to, NC)
            copies.append(
                send(
                    fin.at[yt, :, pl.ds(pl.multiple_of(ct * HALF, HALF), HALF)],
                    gfull.at[:, z, ct, :, pl.ds(pl.multiple_of(mp * COLS, COLS), COLS)],
                    (dp, to),
                )
            )
        keep = local(
            fin.at[y, :, pl.ds(pl.multiple_of(c * HALF, HALF), HALF)],
            gfull.at[:, z, c, :, pl.ds(pl.multiple_of(mp * COLS, COLS), COLS)],
        )
        t = clock["t"] + 3.5
        yield t
        keep.wait()
        for copy in copies:
            copy.wait_recv()

        over, ring = [], {}

        def chunk(h, src):
            return gfull.at[2 * h : 2 * h + 2, src, c]

        for h in (0, 1):
            for d in (1, -1):
                ring[d, h] = send(chunk(h, z), chunk(h, z), zdev(d))
        over.append(send(gfull.at[:, z, c], gfull.at[:, z, c], sibling))
        spawn(deliver(0, lambda xt: gfull.at[xt, z, c], t, 3.0), t)
        spawn(moments(t), t + 8)
        for s in range(4):
            for h in (0, 1):
                yield t + (s + 1) * 3.0 + h * 1.5
                for d in (1, -1):
                    if (d, h) not in ring:
                        continue
                    ring.pop((d, h)).wait_recv()
                    src = lax.rem(z - d * (s + 1) + NZ, NZ)
                    if s < 2 or (s == 2 and (h == 0) == (d == 1)):
                        ring[d, h] = send(chunk(h, src), chunk(h, src), zdev(d))
                    over.append(send(chunk(h, src), chunk(h, src), sibling))
        done.add("gathered")

        rows_of = NX * HALF
        i = lax.broadcasted_iota(jnp.int32, (rows_of, ORDER), 0)
        j = lax.broadcasted_iota(jnp.int32, (rows_of, ORDER), 1)
        wanted = (i // HALF) * (NZ * ROWS) + z * ROWS + c * HALF + lax.rem(i, HALF)
        lhs1[rows_of:] = jnp.where(j == wanted, 1.0, 0.0).astype(bf16)
        lhs1[0:rows_of] = gfull[:, z, c].reshape(rows_of, ORDER)
        for copy in over:
            copy.wait_recv()
        width = NZ * ROWS
        for n in range(NX):
            o = lax.dot_general(
                lhs1[...], gfull[n].reshape(width, ORDER), (((1,), (1,)), ((), ())), preferred_element_type=f32
            )
            res[1, :, :, n * width : (n + 1) * width] = o[0:rows_of].reshape(NX, HALF, width).astype(bf16)
            lhs2[rows_of:, n * width : (n + 1) * width] = o[rows_of:].astype(bf16)
        yield from need("left_roots")
        for n in range(NX):
            o = jnp.dot(
                lhs2[...],
                gfull[:, :, :, :, n * width : (n + 1) * width].reshape(ORDER, width),
                preferred_element_type=f32,
            )
            res[0, :, :, n * width : (n + 1) * width] = o[0:rows_of].reshape(NX, HALF, width).astype(bf16)
            res[2, :, :, n * width : (n + 1) * width] = o[rows_of:].reshape(NX, HALF, width).astype(bf16)
        t = clock["t"] + 3.0
        for r in range(3):
            spawn(deliver(1 + r, lambda xt, r=r: res.at[r, xt], t + 2.0 * r, 3.0), t + 0.01 * r)
        spawn(statistics(2, load_ls, lsv, out_l, left_out), t + 14)
        spawn(statistics(3, load_rs, rsv, out_r, right_out), t + 16)
        yield t + 10
        yield from need(("won", 1), "moments")
        load_r.wait()
        tile = norm_tile["v"]
        for s in range(SLOT_COUNT):
            p = jnp.dot(won[1, s].reshape(ROWS, ORDER), rrv[s], preferred_element_type=f32)
            prec[s] = p.astype(bf16)
            tile = jnp.where(row(SLOT_COUNT + s), jnp.sum(p * p), tile)
        norm_me[...] = tile
        copies_n = [send(norm_me, norm_z.at[k - 1], zdev(k)) for k in range(1, NZ)]
        copies_u = []
        for k in range(1, N_MP):
            to = lax.rem(mp + k, N_MP)
            cols = pl.ds(pl.multiple_of(to * COLS, COLS), COLS)
            copies_u.append(send(prec.at[:, :, cols], upd_in.at[mp], (dp, to)))
        keep = local(prec.at[:, :, pl.ds(pl.multiple_of(mp * COLS, COLS), COLS)], upd_in.at[mp])
        yield clock["t"] + 4.0
        for k, copy in enumerate(copies_n):
            copy.wait_recv()
            tile = tile + norm_z[k]
        norm_me2 = norm_x.at[NX - 1]
        norm_me2[...] = tile
        copies_n = [send(norm_me2, norm_x.at[k - 1], xdev(k)) for k in range(1, NX)]
        yield clock["t"] + 3.0
        for k, copy in enumerate(copies_n):
            copy.wait_recv()
            tile = tile + norm_x[k]
        cells = float(ORDER * ORDER)
        graft = jnp.sqrt(tile[0:SLOT_COUNT] / cells) / jnp.sqrt(tile[SLOT_COUNT:] / cells + graft_eps)
        norm_m[mp] = jnp.concatenate([graft, graft], axis=0)
        copies_n = [send(norm_m.at[mp], norm_m.at[mp], (dp, lax.rem(mp + k, N_MP))) for k in range(1, N_MP)]
        yield clock["t"] + 3.0
        keep.wait()
        for copy in copies_u + copies_n:
            copy.wait_recv()
        for b in range(BLOCKS):
            g = jnp.sum(jnp.where(row(place[b]), norm_m[own[b]], 0.0), axis=0, keepdims=True)
            upd_s[b] = (upd_in[own[b], place[b]].astype(f32) * g).astype(bf16)
        stores.append(local(upd_s, upd_out))

    spawn(main(), 2)
    run()
    for copy in stores:
        copy.wait()
    for copy in sent:
        copy.wait_send()
    assert counts["remote"] <= N_SEMS, counts


def finish(
    upd, left, right, first, second, vec_sum, vec_first, vec_second,
    upd_out, left_out, right_out, first_out, second_out, vec_out, vec_first_out, vec_second_out,
    upd_v, slots_v, in_sems, out_sems,
):
    moves = []
    for n, (src, dst) in enumerate(((left, left_out), (right, right_out), (first, first_out), (second, second_out))):
        for s in range(SLOT_COUNT):
            moves.append((src.at[s], slots_v.at[n, s], dst.at[s]))
    moves.append((upd, upd_v, upd_out))
    loads = [pltpu.make_async_copy(src, held, in_sems.at[i]) for i, (src, held, _) in enumerate(moves)]
    for copy in loads:
        copy.start()
    total = vec_sum[...]
    n1 = beta_one * vec_first[...] + (1.0 - beta_one) * total
    n2 = beta_two * vec_second[...] + (1.0 - beta_two) * total * total
    vec_first_out[...] = n1
    vec_second_out[...] = n2
    vec_out[...] = (n1 / (jnp.sqrt(n2) + adam_eps)).astype(bf16)
    puts = []
    for i, (_, held, dst) in enumerate(moves):
        loads[i].wait()
        puts.append(pltpu.make_async_copy(held, dst, out_sems.at[i]))
        puts[i].start()
    for copy in puts:
        copy.wait()


def body(
    grad_parts, owners, left_stat, right_stat, left_root, right_root, first_moment, second_moment,
    vec_grad, vec_first, vec_second,
):
    hbm = pl.BlockSpec(memory_space=pl.ANY)
    vmem = pl.BlockSpec(memory_space=pltpu.VMEM)
    smem = pl.BlockSpec(memory_space=pltpu.SMEM)
    slots = jax.ShapeDtypeStruct((SLOT_COUNT, ROWS, ORDER), f32)
    vec_rows = vec_grad.shape[1] // COLS
    V = pltpu.VMEM
    scratch = [
        V((NX, NY, NX, NZ, ROWS, COLS), bf16),
        V((2, 2, 4, 2, 2, NX, ROWS, COLS), bf16),
        V((2, 2, 4, NX, ROWS, COLS), bf16),
        V((2, 2, 2, NZ, ROWS, COLS), bf16),
        V((2, 2, 2, NZ, ROWS, COLS), bf16),
        V((2, 2, 2, NZ, ROWS, COLS), bf16),
        V((2, NX, ROWS, COLS), bf16),
        V((2, NX, ROWS, COLS), bf16),
        V((2, NX, ROWS, COLS), bf16),
        V((2, NX, NZ, ROWS, COLS), bf16),
        V((NX, 2, NX, ROWS, COLS), bf16),
        V((NY, NX, ROWS, COLS), bf16),
        V((NX, NZ, NC, HALF, ORDER), bf16),
        V((NY, NC, SLOT_COUNT, HALF, ORDER), bf16),
        V((NX, HALF, ORDER), bf16),
        V((NX, HALF, ORDER), bf16),
        V((2 * NX * HALF, ORDER), bf16),
        V((2 * NX * HALF, ORDER), bf16),
        V((3, NX, HALF, ORDER), bf16),
        *[V((NY, NX, HALF, ORDER), bf16)] * 4,
        V((4, SLOT_COUNT, HALF, ORDER), bf16),
        V((4, SLOT_COUNT, NC, HALF, ORDER), bf16),
        V((SLOT_COUNT, ORDER, ORDER), bf16),
        V((SLOT_COUNT, ROWS, ORDER), f32),
        V((SLOT_COUNT, ROWS, ORDER), f32),
        V((SLOT_COUNT, ROWS, ORDER), f32),
        V((SLOT_COUNT, ROWS, ORDER), f32),
        V((SLOT_COUNT, ROWS, ORDER), f32),
        V((SLOT_COUNT, ROWS, ORDER), f32),
        V((SLOT_COUNT, ROWS, ORDER), f32),
        V((SLOT_COUNT, ROWS, ORDER), f32),
        V((SLOT_COUNT, ROWS, ORDER), bf16),
        V((N_MP, SLOT_COUNT, ROWS, COLS), bf16),
        V((8, COLS), f32),
        V((NZ - 1, 8, COLS), f32),
        V((NX, 8, COLS), f32),
        V((N_MP, 8, COLS), f32),
        V((NX - 1, vec_rows, COLS), f32),
        V((vec_rows, COLS), f32),
        V((NZ - 1, vec_rows, COLS), f32),
        V((BLOCKS, ROWS, COLS), bf16),
        pltpu.SemaphoreType.DMA((N_SEMS,)),
        pltpu.SemaphoreType.DMA((N_SEMS,)),
        pltpu.SemaphoreType.DMA((24,)),
    ]
    block_update, left_new, right_new, first_new, second_new, vec_sum = pl.pallas_call(
        kernel,
        out_shape=(
            jax.ShapeDtypeStruct((BLOCKS, ROWS, COLS), bf16), slots, slots, slots, slots,
            jax.ShapeDtypeStruct((vec_rows, COLS), f32),
        ),
        in_specs=[smem] + [hbm] * 7 + [vmem],
        out_specs=(hbm,) * 5 + (vmem,),
        scratch_shapes=scratch,
        compiler_params=pltpu.CompilerParams(
            collective_id=0, has_side_effects=True, vmem_limit_bytes=62 * 1024 * 1024
        ),
    )(
        owners,
        grad_parts.reshape(NX, NY, NX, NZ, ROWS, COLS),
        left_root.reshape(SLOT_COUNT, NC, HALF, ORDER),
        right_root,
        left_stat,
        right_stat,
        first_moment,
        second_moment,
        vec_grad.astype(f32).reshape(vec_rows, COLS),
    )
    vec_f32 = jax.ShapeDtypeStruct((vec_rows, COLS), f32)
    block_update, left_new, right_new, first_new, second_new, vec_update, vec_first_new, vec_second_new = pl.pallas_call(
        finish,
        out_shape=(
            jax.ShapeDtypeStruct((BLOCKS, ROWS, COLS), bf16), slots, slots, slots, slots,
            jax.ShapeDtypeStruct((vec_rows, COLS), bf16), vec_f32, vec_f32,
        ),
        in_specs=[hbm] * 5 + [vmem] * 3,
        out_specs=(hbm,) * 5 + (vmem,) * 3,
        scratch_shapes=[
            V((BLOCKS, ROWS, COLS), bf16),
            V((4, SLOT_COUNT, ROWS, ORDER), f32),
            pltpu.SemaphoreType.DMA((4 * SLOT_COUNT + 1,)),
            pltpu.SemaphoreType.DMA((4 * SLOT_COUNT + 1,)),
        ],
    )(
        block_update, left_new, right_new, first_new, second_new, vec_sum,
        vec_first.reshape(vec_rows, COLS), vec_second.reshape(vec_rows, COLS),
    )
    return (
        block_update,
        left_new,
        right_new,
        first_new,
        second_new,
        vec_update.reshape(vec_first.shape),
        vec_first_new.reshape(vec_first.shape),
        vec_second_new.reshape(vec_first.shape),
    )


def solution(mesh):
    slots = P("mp", "dp", None)
    return jax.shard_map(
        body,
        mesh=mesh,
        in_specs=(
            P("dp", None, None, "mp"), P(), slots, slots, slots, P("mp", None, None), slots, slots,
            P("dp", "mp"), P("mp"), P("mp"),
        ),
        out_specs=(P(None, "dp", "mp"), slots, slots, slots, slots, P("mp"), P("mp"), P("mp")),
        check_vma=False,
    )
```

```python
import heapq

import jax
import jax.numpy as jnp
from jax import lax
from jax.experimental import pallas as pl
from jax.experimental.pallas import tpu as pltpu
from jax.sharding import PartitionSpec as P

beta_one = 0.9
beta_two = 0.95
adam_eps = 1e-08
graft_eps = 1e-06

MESH = pl.DeviceIdType.MESH
NX, NZ, NY, NC = 4, 8, 4, 2
N_MP = NY * NC
BLOCKS, SLOT_COUNT, ROWS, ORDER, COLS = 16, 4, 32, 1024, 128
HALF = ROWS // NC
N_SEMS = 248
bf16, f32 = jnp.bfloat16, jnp.float32


def kernel(
    owners, grad, lroot, rroot, lstat, rstat, mom1, mom2, vecg,
    upd_out, left_out, right_out, first_out, second_out, vec_out,
    gin, rbz1, rbz2, ra1, rr1, rs1, ra2, rr2, rs2, r1, r2, fin, gfull,
    ly, lsel, lhome, lhs1, lhs2, res, held0, held1, held2, held3, stage, won, rrv, lsv, rsv, m1v, m2v,
    out_l, out_r, out_1, out_2, prec, upd_in, norm_me, norm_z, norm_m, vx, vs, vz, upd_s,
    send_sems, recv_sems, local_sems,
):
    dp, mp = lax.axis_index("dp"), lax.axis_index("mp")
    x, z = dp // NZ, lax.rem(dp, NZ)
    y, c = mp // NC, lax.rem(mp, NC)
    held = (held0, held1, held2, held3)
    counts = {"remote": 0, "local": 0}
    sent = []

    def xdev(k):
        return (lax.rem(x + k + NX, NX) * NZ + z, mp)

    def zdev(k):
        return (x * NZ + lax.rem(z + k + NZ, NZ), mp)

    def ydev(k):
        return (dp, lax.rem(y + k + NY, NY) * NC + c)

    sibling = (dp, y * NC + 1 - c)

    def send(src, dst, device):
        i = counts["remote"]
        counts["remote"] += 1
        copy = pltpu.make_async_remote_copy(
            src_ref=src, dst_ref=dst, send_sem=send_sems.at[i], recv_sem=recv_sems.at[i],
            device_id=device, device_id_type=MESH,
        )
        copy.start()
        sent.append(copy)
        return copy

    def local(src, dst):
        i = counts["local"]
        counts["local"] += 1
        copy = pltpu.make_async_copy(src, dst, local_sems.at[i])
        copy.start()
        return copy

    load_z = local(grad.at[:, 2:4], gin.at[:, 2:4])
    load_x = local(grad.at[:, 0:2], gin.at[:, 0:2])
    load_l = local(lroot.at[:, c], ly.at[y, c])

    barrier = pltpu.get_barrier_semaphore()
    partners = [(lax.rem(dp + k, NX * NZ), mp) for k in range(1, NX * NZ)]
    partners += [(dp, lax.rem(mp + k, N_MP)) for k in range(1, N_MP)]
    for device in partners:
        pl.semaphore_signal(barrier, inc=1, device_id=device, device_id_type=MESH)

    own = [owners[b] for b in range(BLOCKS)]
    slot = []
    for b in range(BLOCKS):
        s = 0
        for a in range(b):
            s = s + jnp.where(own[a] == own[b], 1, 0)
        slot.append(s)
    place = [0] + [jnp.minimum(s, SLOT_COUNT - 1) for s in slot[1:]]

    def picks(who):
        chosen = []
        for s in range(SLOT_COUNT):
            p = jnp.int32(0)
            for b in range(BLOCKS):
                p = p + jnp.where((own[b] == who) & (slot[b] == s), b, 0)
            chosen.append(p)
        return chosen

    mine, theirs = picks(mp), picks(y * NC + 1 - c)
    owned = jnp.int32(0)
    for b in range(BLOCKS):
        owned = owned + jnp.where(own[b] == mp, 1, 0)

    pl.semaphore_wait(barrier, len(partners))

    def accumulate(into, term):
        into[...] = into[...] + term[...]

    queue = []
    clock = {"t": 0.0, "n": 0}
    done = set()

    def spawn(gen, t):
        clock["n"] += 1
        heapq.heappush(queue, (t, clock["n"], gen))

    def run():
        while queue:
            t, _, gen = heapq.heappop(queue)
            clock["t"] = t
            try:
                nxt = next(gen)
            except StopIteration:
                continue
            spawn(gen, nxt)

    def need(*names):
        while not all(n in done for n in names):
            yield clock["t"] + 0.25

    def z_stream(name, d, h, term, rb, t0, dt, origin=None):
        steps = 4 if (h == 0) == (d == 1) else 3
        di = 0 if d == 1 else 1
        copy = send((origin or term)(lax.rem(z + d * steps + NZ, NZ), h), rb.at[di, h, 0], zdev(d))
        for s in range(steps):
            yield t0 + (s + 1) * dt
            copy.wait_recv()
            if s < steps - 1:
                accumulate(rb.at[di, h, s], term(lax.rem(z + d * (steps - 1 - s) + NZ, NZ), h))
                copy = send(rb.at[di, h, s], rb.at[di, h, s + 1], zdev(d))
        done.add((name, d, h))

    def last(d, h):
        return 3 if (h == 0) == (d == 1) else 2

    def x_stream(name, term, ra, rr, rs, put, times, origin=None):
        first, raw, second = {}, {}, {}
        for d, di in ((1, 0), (-1, 1)):
            first[d] = send((origin or term)(lax.rem(x + 2, NX), di), ra.at[di], xdev(d))
        yield times[0]
        for d, di in ((1, 0), (-1, 1)):
            raw[d] = send((origin or term)(lax.rem(x + d + NX, NX), 1 - di), rr.at[di], xdev(d))
        yield times[1]
        for d, di in ((1, 0), (-1, 1)):
            first[d].wait_recv()
            accumulate(ra.at[di], term(lax.rem(x + d + NX, NX), di))
            second[d] = send(ra.at[di], rs.at[di], xdev(d))
        yield times[2]
        for d in (1, -1):
            raw[d].wait_recv()
            second[d].wait_recv()
        put(0, add3(term(x, 0), rs.at[0], rr.at[1]))
        put(1, add3(term(x, 1), rr.at[0], rs.at[1]))
        done.add(name)

    def add3(a, b, d):
        return (a[...].astype(f32) + b[...].astype(f32) + d[...].astype(f32)).astype(bf16)

    def term_z1(Z, h):
        return gin.at[2 * h : 2 * h + 2, 2:4, :, Z]

    def hbm_z1(Z, h):
        return grad.at[2 * h : 2 * h + 2, 2:4, :, Z]

    for d, h in ((1, 0), (-1, 1), (1, 1), (-1, 0)):
        spawn(z_stream("z1", d, h, term_z1, rbz1, 0.5 + 2.8 * ((h == 0) != (d == 1)), 5.6, hbm_z1), 0)

    def x_stage_one(yb):
        def term(X, h):
            return gin.at[X, yb, 2 * h : 2 * h + 2]

        def put(h, value):
            r1[yb, 2 * h : 2 * h + 2] = value

        def origin(X, h):
            return grad.at[X, yb, 2 * h : 2 * h + 2]

        t = 2.8 * yb
        times = (0.1 + yb / 100, 4.6 + t, 16.4 + t)
        return x_stream(("x1", yb), term, ra1.at[yb], rr1.at[yb], rs1.at[yb], put, times, origin)

    for yb in range(2):
        spawn(x_stage_one(yb), 0)

    later = {}

    def loads():
        load_x.wait()
        load_z.wait()
        later["1"] = local(mom1, m1v)
        later["2"] = local(mom2, m2v)
        later["ls"] = local(lstat, lsv)
        later["rs"] = local(rstat, rsv)
        later["r"] = local(rroot, rrv)
        yield from ()

    spawn(loads(), 2.0)

    def z_stage_two(yb):
        yield 16.0
        yield from need(("x1", yb))
        t = clock["t"]

        def term(Z, h):
            return r1.at[h, :, Z]

        for d in (1, -1):
            spawn(z_stream("z2", d, yb, term, rbz2, t, 2.4), t)
        yield t + 0.1
        yield from need(("z2", 1, yb), ("z2", -1, yb))
        fin[yb] = add3(r1.at[yb, :, z], rbz2.at[0, yb, last(1, yb)], rbz2.at[1, yb, last(-1, yb)])
        done.add(("fin", yb))

    for yb in range(2):
        spawn(z_stage_two(yb), 1)

    def x_stage_two():
        yield 20.0
        for h in (0, 1):
            yield from need(("z1", 1, h), ("z1", -1, h))
            r2[2 * h : 2 * h + 2] = add3(
                gin.at[2 * h : 2 * h + 2, 2:4, :, z], rbz1.at[0, h, last(1, h)], rbz1.at[1, h, last(-1, h)]
            )

        def term(X, h):
            return r2.at[X, h]

        def put(h, value):
            fin[2 + h] = value

        t = clock["t"]
        yield from x_stream("x2", term, ra2, rr2, rs2, put, (t, t + 2.4, t + 4.8))

    spawn(x_stage_two(), 1)

    def left_roots():
        got = send(lroot.at[:, 1 - c], ly.at[y, c], sibling)
        yield 3.0
        load_l.wait()
        got.wait_recv()
        copies = {}
        for d in (1, -1):
            copies[d] = send(ly.at[y], ly.at[y], ydev(d))
        yield 12.0
        relays = []
        for d, oc in ((1, 0), (-1, 1)):
            copies[d].wait_recv()
            frm = lax.rem(y - d + NY, NY)
            relays.append(send(ly.at[frm, oc], ly.at[frm, oc], ydev(d)))
        yield 18.5
        for copy in relays:
            copy.wait_recv()
        for xb in range(NX):
            o, s = jnp.int32(0), jnp.int32(0)
            for yb in range(NY):
                o = o + jnp.where(y == yb, own[NY * xb + yb], 0)
                s = s + jnp.where(y == yb, place[NY * xb + yb], 0)
            lsel[xb] = ly[o // NC, lax.rem(o, NC), s]
        copies = []
        for k in range(1, NX):
            copies.append(send(lsel.at[lax.rem(x + k, NX)], lhome.at[x], xdev(k)))
        lhome[x] = lsel[x]
        yield 26.0
        for copy in copies:
            copy.wait_recv()
        lhs2[0 : NX * HALF] = lhome[...].reshape(NX * HALF, ORDER)
        done.add("left_roots")

    spawn(left_roots(), 0.6)

    def deliver(t, src, t0, hop):
        copies = []
        for k in range(1, NX):
            copies.append(send(src(lax.rem(x + k, NX)), held[t].at[y, x], xdev(k)))
        keep = local(src(x), held[t].at[y, x])
        yield t0 + hop
        keep.wait()
        for copy in copies:
            copy.wait_recv()
        copies = {}
        for d in (1, -1):
            copies[d] = send(held[t].at[y], held[t].at[y], ydev(d))
        yield t0 + 2.5 * hop
        relays = []
        for d, hb in ((1, 0), (-1, 1)):
            copies[d].wait_recv()
            frm = lax.rem(y - d + NY, NY)
            part = held[t].at[frm, 2 * hb : 2 * hb + 2]
            relays.append(send(part, part, ydev(d)))
        yield t0 + 3.5 * hop
        for copy in relays:
            copy.wait_recv()
        for s in range(SLOT_COUNT):
            b = theirs[s]
            stage[t, s] = held[t][lax.rem(b, NY), b // NY]
        got = send(stage.at[t], won.at[t, :, c], sibling)
        for s in range(SLOT_COUNT):
            b = mine[s]
            won[t, s, c] = held[t][lax.rem(b, NY), b // NY]
        yield t0 + 4 * hop
        got.wait_recv()
        done.add(("won", t))

    def used(s):
        return jnp.full((ROWS, ORDER), owned, jnp.int32) > s

    def row(s):
        return lax.broadcasted_iota(jnp.int32, (8, COLS), 0) == s

    def slot_rows(t, s):
        return won[t, s].reshape(ROWS, ORDER).astype(f32)

    norm_tile = {"v": jnp.zeros((8, COLS), f32)}
    stores = []

    def moments(t0):
        yield from need(("won", 0))
        later["1"].wait()
        later["2"].wait()
        for s in range(SLOT_COUNT):
            g = slot_rows(0, s)
            m1, m2 = m1v[s], m2v[s]
            n1 = jnp.where(used(s), beta_one * m1 + (1.0 - beta_one) * g, m1)
            n2 = jnp.where(used(s), beta_two * m2 + (1.0 - beta_two) * g * g, m2)
            out_1[s] = n1
            out_2[s] = n2
            adam = n1 / (jnp.sqrt(n2) + adam_eps)
            norm_tile["v"] = jnp.where(row(s), jnp.sum(adam * adam), norm_tile["v"])
        stores.append(local(out_1, first_out))
        stores.append(local(out_2, second_out))
        done.add("moments")

    def statistics(t, load, stat, out, dst):
        yield from need(("won", t))
        later[load].wait()
        for s in range(SLOT_COUNT):
            old = stat[s]
            out[s] = jnp.where(used(s), old + slot_rows(t, s) * (1.0 / ORDER), old)
        stores.append(local(out, dst))

    def vectors():
        copies = [send(vecg, vx.at[k - 1], xdev(k)) for k in range(1, NX)]
        yield 15.0
        for copy in copies:
            copy.wait_recv()
        vs[...] = vecg[...] + vx[0] + vx[1] + vx[2]
        yield 48.0
        yield from need("gathered")
        copies = [send(vs, vz.at[k - 1], zdev(k)) for k in range(1, NZ)]
        yield clock["t"] + 12.0
        total = vs[...]
        for k, copy in enumerate(copies):
            copy.wait_recv()
            total = total + vz[k]
        vec_out[...] = total

    spawn(vectors(), 0.7)

    def main():
        yield 22.0
        yield from need(("fin", 0), ("fin", 1), "x2")
        copies = []
        for k in range(1, N_MP):
            to = lax.rem(mp + k, N_MP)
            yt, ct = to // NC, lax.rem(to, NC)
            copies.append(
                send(
                    fin.at[yt, :, pl.ds(pl.multiple_of(ct * HALF, HALF), HALF)],
                    gfull.at[:, z, ct, :, pl.ds(pl.multiple_of(mp * COLS, COLS), COLS)],
                    (dp, to),
                )
            )
        keep = local(
            fin.at[y, :, pl.ds(pl.multiple_of(c * HALF, HALF), HALF)],
            gfull.at[:, z, c, :, pl.ds(pl.multiple_of(mp * COLS, COLS), COLS)],
        )
        t = clock["t"] + 3.5
        yield t
        keep.wait()
        for copy in copies:
            copy.wait_recv()

        over, ring = [], {}

        def chunk(h, src):
            return gfull.at[2 * h : 2 * h + 2, src, c]

        for h in (0, 1):
            for d in (1, -1):
                ring[d, h] = send(chunk(h, z), chunk(h, z), zdev(d))
        over.append(send(gfull.at[:, z, c], gfull.at[:, z, c], sibling))
        spawn(deliver(0, lambda xt: gfull.at[xt, z, c], t, 3.0), t)
        spawn(moments(t), t + 8)
        for s in range(4):
            for h in (0, 1):
                yield t + (s + 1) * 3.0 + h * 1.5
                for d in (1, -1):
                    if (d, h) not in ring:
                        continue
                    ring.pop((d, h)).wait_recv()
                    src = lax.rem(z - d * (s + 1) + NZ, NZ)
                    if s < 2 or (s == 2 and (h == 0) == (d == 1)):
                        ring[d, h] = send(chunk(h, src), chunk(h, src), zdev(d))
                    over.append(send(chunk(h, src), chunk(h, src), sibling))
        done.add("gathered")

        rows_of = NX * HALF
        i = lax.broadcasted_iota(jnp.int32, (rows_of, ORDER), 0)
        j = lax.broadcasted_iota(jnp.int32, (rows_of, ORDER), 1)
        wanted = (i // HALF) * (NZ * ROWS) + z * ROWS + c * HALF + lax.rem(i, HALF)
        lhs1[rows_of:] = jnp.where(j == wanted, 1.0, 0.0).astype(bf16)
        lhs1[0:rows_of] = gfull[:, z, c].reshape(rows_of, ORDER)
        for copy in over:
            copy.wait_recv()
        width = NZ * ROWS
        for n in range(NX):
            o = lax.dot_general(
                lhs1[...], gfull[n].reshape(width, ORDER), (((1,), (1,)), ((), ())), preferred_element_type=f32
            )
            res[1, :, :, n * width : (n + 1) * width] = o[0:rows_of].reshape(NX, HALF, width).astype(bf16)
            lhs2[rows_of:, n * width : (n + 1) * width] = o[rows_of:].astype(bf16)
        yield from need("left_roots")
        for n in range(NX):
            o = jnp.dot(
                lhs2[...],
                gfull[:, :, :, :, n * width : (n + 1) * width].reshape(ORDER, width),
                preferred_element_type=f32,
            )
            res[0, :, :, n * width : (n + 1) * width] = o[0:rows_of].reshape(NX, HALF, width).astype(bf16)
            res[2, :, :, n * width : (n + 1) * width] = o[rows_of:].reshape(NX, HALF, width).astype(bf16)
        t = clock["t"] + 3.0
        for r in range(3):
            spawn(deliver(1 + r, lambda xt, r=r: res.at[r, xt], t + 2.0 * r, 3.0), t + 0.01 * r)
        spawn(statistics(2, "ls", lsv, out_l, left_out), t + 14)
        spawn(statistics(3, "rs", rsv, out_r, right_out), t + 16)
        yield t + 10
        yield from need(("won", 1), "moments")
        later["r"].wait()
        tile = norm_tile["v"]
        for s in range(SLOT_COUNT):
            p = jnp.dot(won[1, s].reshape(ROWS, ORDER), rrv[s], preferred_element_type=f32)
            prec[s] = p.astype(bf16)
            tile = jnp.where(row(SLOT_COUNT + s), jnp.sum(p * p), tile)
        norm_me[...] = tile
        copies_n = [send(norm_me, norm_z.at[k - 1], (lax.rem(dp + k, NX * NZ), mp)) for k in range(1, NX * NZ)]
        copies_u = []
        for k in range(1, N_MP):
            to = lax.rem(mp + k, N_MP)
            cols = pl.ds(pl.multiple_of(to * COLS, COLS), COLS)
            copies_u.append(send(prec.at[:, :, cols], upd_in.at[mp], (dp, to)))
        keep = local(prec.at[:, :, pl.ds(pl.multiple_of(mp * COLS, COLS), COLS)], upd_in.at[mp])
        yield clock["t"] + 4.0
        for k, copy in enumerate(copies_n):
            copy.wait_recv()
            tile = tile + norm_z[k]
        cells = float(ORDER * ORDER)
        graft = jnp.sqrt(tile[0:SLOT_COUNT] / cells) / jnp.sqrt(tile[SLOT_COUNT:] / cells + graft_eps)
        norm_m[mp] = jnp.concatenate([graft, graft], axis=0)
        copies_n = [send(norm_m.at[mp], norm_m.at[mp], (dp, lax.rem(mp + k, N_MP))) for k in range(1, N_MP)]
        yield clock["t"] + 3.0
        keep.wait()
        for copy in copies_u + copies_n:
            copy.wait_recv()
        for b in range(BLOCKS):
            g = jnp.sum(jnp.where(row(place[b]), norm_m[own[b]], 0.0), axis=0, keepdims=True)
            upd_s[b] = (upd_in[own[b], place[b]].astype(f32) * g).astype(bf16)
        stores.append(local(upd_s, upd_out))

    spawn(main(), 2)
    run()
    for copy in stores:
        copy.wait()
    for copy in sent:
        copy.wait_send()
    assert counts["remote"] <= N_SEMS, counts


def finish(
    upd, left, right, first, second, vec_sum, vec_first, vec_second,
    upd_out, left_out, right_out, first_out, second_out, vec_out, vec_first_out, vec_second_out,
    upd_v, slots_v, in_sems, out_sems,
):
    moves = []
    for n, (src, dst) in enumerate(((left, left_out), (right, right_out), (first, first_out), (second, second_out))):
        for s in range(SLOT_COUNT):
            moves.append((src.at[s], slots_v.at[n, s], dst.at[s]))
    moves.append((upd, upd_v, upd_out))
    loads = [pltpu.make_async_copy(src, held, in_sems.at[i]) for i, (src, held, _) in enumerate(moves)]
    for copy in loads:
        copy.start()
    total = vec_sum[...]
    n1 = beta_one * vec_first[...] + (1.0 - beta_one) * total
    n2 = beta_two * vec_second[...] + (1.0 - beta_two) * total * total
    vec_first_out[...] = n1
    vec_second_out[...] = n2
    vec_out[...] = (n1 / (jnp.sqrt(n2) + adam_eps)).astype(bf16)
    puts = []
    for i, (_, held, dst) in enumerate(moves):
        loads[i].wait()
        puts.append(pltpu.make_async_copy(held, dst, out_sems.at[i]))
        puts[i].start()
    for copy in puts:
        copy.wait()


def body(
    grad_parts, owners, left_stat, right_stat, left_root, right_root, first_moment, second_moment,
    vec_grad, vec_first, vec_second,
):
    hbm = pl.BlockSpec(memory_space=pl.ANY)
    vmem = pl.BlockSpec(memory_space=pltpu.VMEM)
    smem = pl.BlockSpec(memory_space=pltpu.SMEM)
    slots = jax.ShapeDtypeStruct((SLOT_COUNT, ROWS, ORDER), f32)
    vec_rows = vec_grad.shape[1] // COLS
    V = pltpu.VMEM
    scratch = [
        V((NX, NY, NX, NZ, ROWS, COLS), bf16),
        V((2, 2, 4, 2, 2, NX, ROWS, COLS), bf16),
        V((2, 2, 4, NX, ROWS, COLS), bf16),
        V((2, 2, 2, NZ, ROWS, COLS), bf16),
        V((2, 2, 2, NZ, ROWS, COLS), bf16),
        V((2, 2, 2, NZ, ROWS, COLS), bf16),
        V((2, NX, ROWS, COLS), bf16),
        V((2, NX, ROWS, COLS), bf16),
        V((2, NX, ROWS, COLS), bf16),
        V((2, NX, NZ, ROWS, COLS), bf16),
        V((NX, 2, NX, ROWS, COLS), bf16),
        V((NY, NX, ROWS, COLS), bf16),
        V((NX, NZ, NC, HALF, ORDER), bf16),
        V((NY, NC, SLOT_COUNT, HALF, ORDER), bf16),
        V((NX, HALF, ORDER), bf16),
        V((NX, HALF, ORDER), bf16),
        V((2 * NX * HALF, ORDER), bf16),
        V((2 * NX * HALF, ORDER), bf16),
        V((3, NX, HALF, ORDER), bf16),
        *[V((NY, NX, HALF, ORDER), bf16)] * 4,
        V((4, SLOT_COUNT, HALF, ORDER), bf16),
        V((4, SLOT_COUNT, NC, HALF, ORDER), bf16),
        V((SLOT_COUNT, ORDER, ORDER), bf16),
        V((SLOT_COUNT, ROWS, ORDER), f32),
        V((SLOT_COUNT, ROWS, ORDER), f32),
        V((SLOT_COUNT, ROWS, ORDER), f32),
        V((SLOT_COUNT, ROWS, ORDER), f32),
        V((SLOT_COUNT, ROWS, ORDER), f32),
        V((SLOT_COUNT, ROWS, ORDER), f32),
        V((SLOT_COUNT, ROWS, ORDER), f32),
        V((SLOT_COUNT, ROWS, ORDER), f32),
        V((SLOT_COUNT, ROWS, ORDER), bf16),
        V((N_MP, SLOT_COUNT, ROWS, COLS), bf16),
        V((8, COLS), f32),
        V((NX * NZ - 1, 8, COLS), f32),
        V((N_MP, 8, COLS), f32),
        V((NX - 1, vec_rows, COLS), f32),
        V((vec_rows, COLS), f32),
        V((NZ - 1, vec_rows, COLS), f32),
        V((BLOCKS, ROWS, COLS), bf16),
        pltpu.SemaphoreType.DMA((N_SEMS,)),
        pltpu.SemaphoreType.DMA((N_SEMS,)),
        pltpu.SemaphoreType.DMA((24,)),
    ]
    block_update, left_new, right_new, first_new, second_new, vec_sum = pl.pallas_call(
        kernel,
        out_shape=(
            jax.ShapeDtypeStruct((BLOCKS, ROWS, COLS), bf16), slots, slots, slots, slots,
            jax.ShapeDtypeStruct((vec_rows, COLS), f32),
        ),
        in_specs=[smem] + [hbm] * 7 + [vmem],
        out_specs=(hbm,) * 5 + (vmem,),
        scratch_shapes=scratch,
        compiler_params=pltpu.CompilerParams(
            collective_id=0, has_side_effects=True, vmem_limit_bytes=62 * 1024 * 1024
        ),
    )(
        owners,
        grad_parts.reshape(NX, NY, NX, NZ, ROWS, COLS),
        left_root.reshape(SLOT_COUNT, NC, HALF, ORDER),
        right_root,
        left_stat,
        right_stat,
        first_moment,
        second_moment,
        vec_grad.astype(f32).reshape(vec_rows, COLS),
    )
    vec_f32 = jax.ShapeDtypeStruct((vec_rows, COLS), f32)
    block_update, left_new, right_new, first_new, second_new, vec_update, vec_first_new, vec_second_new = pl.pallas_call(
        finish,
        out_shape=(
            jax.ShapeDtypeStruct((BLOCKS, ROWS, COLS), bf16), slots, slots, slots, slots,
            jax.ShapeDtypeStruct((vec_rows, COLS), bf16), vec_f32, vec_f32,
        ),
        in_specs=[hbm] * 5 + [vmem] * 3,
        out_specs=(hbm,) * 5 + (vmem,) * 3,
        scratch_shapes=[
            V((BLOCKS, ROWS, COLS), bf16),
            V((4, SLOT_COUNT, ROWS, ORDER), f32),
            pltpu.SemaphoreType.DMA((4 * SLOT_COUNT + 1,)),
            pltpu.SemaphoreType.DMA((4 * SLOT_COUNT + 1,)),
        ],
    )(
        block_update, left_new, right_new, first_new, second_new, vec_sum,
        vec_first.reshape(vec_rows, COLS), vec_second.reshape(vec_rows, COLS),
    )
    return (
        block_update,
        left_new,
        right_new,
        first_new,
        second_new,
        vec_update.reshape(vec_first.shape),
        vec_first_new.reshape(vec_first.shape),
        vec_second_new.reshape(vec_first.shape),
    )


def solution(mesh):
    slots = P("mp", "dp", None)
    return jax.shard_map(
        body,
        mesh=mesh,
        in_specs=(
            P("dp", None, None, "mp"), P(), slots, slots, slots, P("mp", None, None), slots, slots,
            P("dp", "mp"), P("mp"), P("mp"),
        ),
        out_specs=(P(None, "dp", "mp"), slots, slots, slots, slots, P("mp"), P("mp"), P("mp")),
        check_vma=False,
    )
```
